256 devices in a mesh: wide: 32 (over x, z_hi, core), narrow: 8 (over y, z_lo).
Axes of the slice: x: 4, y: 4, z: 8 (z_hi: 4, z_lo: 2; z = z_hi * 2 + z_lo), core: 2. Of those that a mesh axis runs over, the one named last changes fastest.
Arguments:
- state_real: float32 [8, 32, 4096, 128], P('narrow', 'wide'), may hold values from -6 to 6
- state_imag: float32 [8, 32, 4096, 128], P('narrow', 'wide'), may hold values from -6 to 6
- gates: float32 [3, 2, 128, 128], replicated, may hold values from -0.375 to 0.375
- gate_orders: int32 [3, 7], replicated, may hold values from 0 to 6, each once within a row
- phase_masks: int32 [8, 2], replicated, may hold values from 1 to 67108864, as said below
- phase_angles: float32 [8], replicated, may hold values from -3.140625 to 3.140625
Outputs:
- out_real: float32 [8, 32, 4096, 128], P('narrow', 'wide')
- out_imag: float32 [8, 32, 4096, 128], P('narrow', 'wide')
The draws below stay inside these ranges and needn't reach their ends.
Inputs may be any that keep to these rules, and one draw needn't show every extreme that they name: `phase_masks`: each entry is 2**q for one qubit q of the whole index of 134217728 amplitudes; the two entries of a row differ.
All inputs are finite; a program needn't handle non-finite values.
Results may differ from the reference program's by a relative error of at most 0.0003.
Values sent between devices are 32-bit elements; how exact they have to be, the bound alone decides.
No kernel may reach another device: no remote copies, remote signals or barrier semaphores. Data moves between devices by JAX's collectives and lax.ppermute only.
A program may use at most 64 MiB of HBM per device.

```python
import jax
import jax.numpy as jnp
from jax import lax

QG = 7
GATE = 128
LAYERS = 3
PAIRS = 8
HI = 4096
NAR = 8
WID = 32
AMPS = 134217728


def draw_phase_masks(key, part):
    qubit_count = int(AMPS).bit_length() - 1
    leading = jax.random.randint(jax.random.fold_in(key, 11), (PAIRS,), 0, qubit_count)
    spacing = jax.random.randint(jax.random.fold_in(key, 12), (PAIRS,), 1, qubit_count)
    trailing = (leading + spacing) % qubit_count
    leading = leading.at[0].set(qubit_count - 1)
    trailing = trailing.at[0].set(0)
    single = jnp.ones((PAIRS,), jnp.int32)
    return jnp.stack([jnp.left_shift(single, leading), jnp.left_shift(single, trailing)], axis=1).astype(jnp.int32)


def level_of(stream_key, extent, cuts, least, high):
    def one(dim, parts):
        draws = jax.random.uniform(jax.random.fold_in(jax.random.fold_in(stream_key, 6), dim), (parts,), jnp.float32, least / len(cuts), high / len(cuts))
        return jnp.repeat(jnp.exp(draws), extent[dim] // parts).reshape((-1,) + (1,) * (len(extent) - dim - 1))

    factor_of = one(*cuts[0])
    for cut in cuts[1:]:
        factor_of = factor_of * one(*cut)
    return factor_of


def centred(own_key, extent, deviation, bound, shards=(), kind=jnp.bfloat16):
    entries = deviation * jax.random.normal(own_key, extent, jnp.float32)
    if shards:
        entries = entries * level_of(own_key, extent, shards, -0.22, 0.18)
    return jnp.clip(entries, -bound, bound).astype(kind)


def setup_inputs(seed: int = 0) -> dict:
    keys = jax.random.split(jax.random.key(seed), 7)
    return {
        "state_real": centred(keys[0], (NAR, WID, HI, GATE), 1.0, 6.0, ((0, 8), (1, 32)), jnp.float32),
        "state_imag": centred(keys[1], (NAR, WID, HI, GATE), 1.0, 6.0, ((0, 8), (1, 32)), jnp.float32),
        "gates": centred(keys[2], (LAYERS, 2, GATE, GATE), (2 * GATE) ** -0.5, 0.375, (), jnp.float32),
        "gate_orders": jax.vmap(lambda own: jax.random.permutation(own, QG))(jax.random.split(keys[3], LAYERS)).reshape((LAYERS, QG)).astype(jnp.int32),
        "phase_masks": draw_phase_masks(jax.random.fold_in(keys[6], 71), 0),
        "phase_angles": jnp.clip(jax.random.uniform(keys[5], (PAIRS,), jnp.float32, -3.140625, 3.140625), -3.140625, 3.140625),
    }


precise = lax.Precision.HIGHEST


def ordered_gate(gate_pair, order_row):
    count = order_row.shape[0]
    states = jnp.arange(2 ** count, dtype=jnp.int32)
    places = jnp.arange(count, dtype=jnp.int32)
    digits = (states[:, None] >> places[None, :]) & 1
    mapped = jnp.sum(digits << order_row[None, :], axis=1)
    permute = (mapped[:, None] == states[None, :]).astype(jnp.float32)
    real_gate = jnp.dot(jnp.dot(permute, gate_pair[0], precision=precise), permute.T, precision=precise)
    imag_gate = jnp.dot(jnp.dot(permute, gate_pair[1], precision=precise), permute.T, precision=precise)
    return real_gate, imag_gate


def mixing(gate_real, gate_imag, real_part, imag_part):
    out_real = jnp.dot(gate_real, real_part, precision=precise) - jnp.dot(gate_imag, imag_part, precision=precise)
    out_imag = jnp.dot(gate_real, imag_part, precision=precise) + jnp.dot(gate_imag, real_part, precision=precise)
    return out_real, out_imag


def phase_turn(real_part, imag_part, flat, phase_masks, phase_angles):
    angle_sum = jnp.zeros(real_part.shape, jnp.float32)
    for which in range(phase_masks.shape[0]):
        both = ((flat & phase_masks[which, 0]) != 0) & ((flat & phase_masks[which, 1]) != 0)
        angle_sum = angle_sum + jnp.where(both, phase_angles[which], 0.0)
    cosine = jnp.cos(angle_sum)
    sine = jnp.sin(angle_sum)
    return real_part * cosine - imag_part * sine, real_part * sine + imag_part * cosine


def reference(state_real, state_imag, gates, gate_orders, phase_masks, phase_angles):
    first_gate = ordered_gate(gates[0], gate_orders[0])
    second_gate = ordered_gate(gates[1], gate_orders[1])
    third_gate = ordered_gate(gates[2], gate_orders[2])
    narrow_count, wide_count, row_count, columns = state_real.shape
    gate_size = first_gate[0].shape[0]

    def front(item):
        position, real_part, imag_part = item
        real_rows = real_part.reshape(-1, columns)
        imag_rows = imag_part.reshape(-1, columns)
        new_real = jnp.dot(real_rows, first_gate[0].T, precision=precise) - jnp.dot(imag_rows, first_gate[1].T, precision=precise)
        new_imag = jnp.dot(imag_rows, first_gate[0].T, precision=precise) + jnp.dot(real_rows, first_gate[1].T, precision=precise)
        flat = position * (wide_count * row_count * columns) + jnp.arange(wide_count * row_count, dtype=jnp.int32)[:, None] * columns + jnp.arange(columns, dtype=jnp.int32)[None, :]
        turned_real, turned_imag = phase_turn(new_real, new_imag, flat, phase_masks, phase_angles)
        mixed_real, mixed_imag = mixing(second_gate[0], second_gate[1], turned_real.reshape(gate_size, -1), turned_imag.reshape(gate_size, -1))
        return mixed_real.reshape(wide_count, row_count, columns), mixed_imag.reshape(wide_count, row_count, columns)

    middle_real, middle_imag = lax.map(front, (jnp.arange(narrow_count, dtype=jnp.int32), state_real, state_imag))

    def finish(item):
        real_part, imag_part = item
        mixed_real, mixed_imag = mixing(third_gate[0], third_gate[1], real_part.reshape(gate_size, -1), imag_part.reshape(gate_size, -1))
        return mixed_real.reshape(real_part.shape), mixed_imag.reshape(imag_part.shape)

    final_real, final_imag = lax.map(finish, (jnp.moveaxis(middle_real, 1, 0), jnp.moveaxis(middle_imag, 1, 0)))
    return jnp.moveaxis(final_real, 0, 1), jnp.moveaxis(final_imag, 0, 1)
```

```python
import jax
import jax.numpy as jnp
from jax import lax
from jax.sharding import PartitionSpec as P

precise = lax.Precision.HIGHEST
close = lax.Precision.HIGH
AXES = ("wide", "narrow")


def ordered_gate(gate_pair, order_row):
    count = order_row.shape[0]
    states = jnp.arange(2**count, dtype=jnp.int32)
    places = jnp.arange(count, dtype=jnp.int32)
    digits = states[:, None] >> places[None, :] & 1
    mapped = jnp.sum(digits << order_row[None, :], axis=1)
    permute = (mapped[:, None] == states[None, :]).astype(jnp.float32)
    real_gate = jnp.dot(
        jnp.dot(permute, gate_pair[0], precision=precise), permute.T, precision=precise
    )
    imag_gate = jnp.dot(
        jnp.dot(permute, gate_pair[1], precision=precise), permute.T, precision=precise
    )
    return (real_gate, imag_gate)


def stacked(gate):
    return jnp.concatenate(
        [
            jnp.concatenate([gate[0], -gate[1]], axis=1),
            jnp.concatenate([gate[1], gate[0]], axis=1),
        ],
        axis=0,
    )


def phase_turn(real_part, imag_part, flat, phase_masks, phase_angles):
    angle_sum = jnp.zeros(real_part.shape, jnp.float32)
    for which in range(phase_masks.shape[0]):
        both = (flat & phase_masks[which, 0] != 0) & (flat & phase_masks[which, 1] != 0)
        angle_sum = angle_sum + jnp.where(both, phase_angles[which], 0.0)
    cosine = jnp.cos(angle_sum)
    sine = jnp.sin(angle_sum)
    return (real_part * cosine - imag_part * sine, real_part * sine + imag_part * cosine)


def body(state_real, state_imag, gates, gate_orders, phase_masks, phase_angles):
    real_part = state_real[0, 0]
    imag_part = state_imag[0, 0]
    rows, columns = real_part.shape
    first = ordered_gate(gates[0], gate_orders[0])
    second = stacked(ordered_gate(gates[1], gate_orders[1]))
    third = stacked(ordered_gate(gates[2], gate_orders[2]))
    both = jnp.concatenate([real_part, imag_part], axis=1)
    new = jnp.dot(both, stacked(first).T, precision=close)
    wide_count = lax.axis_size("wide")
    narrow_count = lax.axis_size("narrow")
    devices = wide_count * narrow_count
    high = rows // devices
    offset = (lax.axis_index("narrow") * wide_count + lax.axis_index("wide")) * (rows * columns)
    flat = (
        offset
        + jnp.arange(rows, dtype=jnp.int32)[:, None] * columns
        + jnp.arange(columns, dtype=jnp.int32)[None, :]
    )
    turned = phase_turn(new[:, :columns], new[:, columns:], flat, phase_masks, phase_angles)
    send = jnp.stack(turned).reshape(2, high, devices, columns).transpose(2, 0, 1, 3)
    got = lax.all_to_all(send, AXES, split_axis=0, concat_axis=0, tiled=True)
    inner = 128 // wide_count
    rest = high // inner
    view = got.reshape(wide_count, narrow_count, 2, inner, rest, columns)
    mid = jnp.dot(
        second, view.transpose(2, 0, 3, 1, 4, 5).reshape(256, -1), precision=close
    )
    mid = mid.reshape(2, wide_count, inner, narrow_count, rest, columns)
    out = jnp.dot(
        third, mid.transpose(0, 3, 2, 4, 1, 5).reshape(256, -1), precision=close
    )
    back = out.reshape(2, narrow_count, high, wide_count, columns).transpose(3, 1, 0, 2, 4)
    ret = lax.all_to_all(
        back.reshape(devices, 2, high, columns), AXES, split_axis=0, concat_axis=0, tiled=True
    )
    final = ret.transpose(1, 2, 0, 3).reshape(2, rows, columns)
    return (final[0][None, None], final[1][None, None])


def solution(mesh):
    placed = (P("narrow", "wide", None, None), P("narrow", "wide", None, None), P(), P(), P(), P())
    return jax.shard_map(
        body,
        mesh=mesh,
        in_specs=placed,
        out_specs=(P("narrow", "wide", None, None), P("narrow", "wide", None, None)),
        check_vma=False,
    )
```

```python
import functools

import jax
import jax.numpy as jnp
from jax import lax
from jax.experimental import pallas as pl
from jax.experimental.pallas import tpu as pltpu
from jax.sharding import PartitionSpec as P

AXES = ("wide", "narrow")
QUBITS = 7
GATE = 128
f32 = jnp.float32
bf16 = jnp.bfloat16
VMEM = pl.BlockSpec(memory_space=pltpu.VMEM)
SMEM = pl.BlockSpec(memory_space=pltpu.SMEM)


def halves(value):
    high = value.astype(bf16)
    return high, (value - high.astype(f32)).astype(bf16)


def mul(left, right):
    return jnp.dot(left, right, preferred_element_type=f32)


def pick(states, orders_ref, row):
    mapped = jnp.zeros_like(states)
    for place in range(QUBITS):
        mapped = mapped + (((states >> place) & 1) << orders_ref[row, place])
    return (mapped == lax.broadcasted_iota(jnp.int32, (GATE, GATE), 1)).astype(bf16)


def chosen(left, right, gate):
    out = []
    for part in halves(gate):
        rows = mul(left, part).astype(bf16)
        out.append(
            lax.dot_general(rows, right, (((1,), (1,)), ((), ())), preferred_element_type=f32)
            .astype(bf16)
        )
    return out


def sincos(angle):
    turns = jnp.floor(angle * 0.6366197723675814 + 0.5)
    r = angle - turns * 1.5703125
    r = r - turns * 4.8351287841796875e-4
    r = r - turns * 3.13855707645416e-7
    s = r * r
    sine = r + r * s * (-1.6666654611e-1 + s * (8.3321608736e-3 - s * 1.9515295891e-4))
    cosine = 1.0 - 0.5 * s + s * s * (
        4.166664568298827e-2 + s * (-1.388731625493765e-3 + s * 2.443315711809948e-5)
    )
    quarter = turns.astype(jnp.int32)
    swap = (quarter & 1) == 1
    base_sin = jnp.where(swap, cosine, sine)
    base_cos = jnp.where(swap, sine, cosine)
    sine = jnp.where((quarter & 2) == 2, -base_sin, base_sin)
    cosine = jnp.where(((quarter + 1) & 2) == 2, -base_cos, base_cos)
    return sine, cosine


def front_kernel(base_ref, orders_ref, masks_ref, angles_ref, real_ref, imag_ref, gates_ref,
                 send_ref, high_ref, low_ref):
    devices = real_ref.shape[0] // 16
    states = lax.broadcasted_iota(jnp.int32, (GATE, GATE), 0)
    one_hot = pick(states, orders_ref, 0)
    real_high, real_low = chosen(one_hot, one_hot, gates_ref[0, 0])
    imag_high, imag_low = chosen(one_hot, one_hot, gates_ref[0, 1])
    for ref, real, imag in ((high_ref, real_high, imag_high), (low_ref, real_low, imag_low)):
        ref[:GATE, :GATE] = real
        ref[:GATE, GATE:] = -imag
        ref[GATE:, :GATE] = imag
        ref[GATE:, GATE:] = real

    def turned(left, right):
        return lax.dot_general(left, right, (((1,), (1,)), ((), ())), preferred_element_type=f32)

    shape = (devices, GATE)
    within = (
        lax.broadcasted_iota(jnp.int32, shape, 0) * GATE
        + lax.broadcasted_iota(jnp.int32, shape, 1)
    )

    @pl.loop(0, 16)
    def _(top):
        rows = pl.ds(pl.multiple_of(top * devices, devices), devices)
        both = jnp.concatenate([real_ref[rows, :], imag_ref[rows, :]], axis=1)
        x_high, x_low = halves(both)
        new = (
            turned(x_high, high_ref[...])
            + turned(x_high, low_ref[...])
            + turned(x_low, high_ref[...])
        )
        flat = within + (base_ref[0] + top * (devices * GATE))
        angle = jnp.zeros(shape, f32)
        for pair in range(masks_ref.shape[0]):
            mask = masks_ref[pair, 0] | masks_ref[pair, 1]
            angle = angle + jnp.where((flat & mask) == mask, angles_ref[pair], 0.0)
        sine, cosine = sincos(angle)
        real = new[:, :GATE]
        imag = new[:, GATE:]
        send_ref[pl.ds(top, devices, stride=32), :] = real * cosine - imag * sine
        send_ref[pl.ds(top + 16, devices, stride=32), :] = real * sine + imag * cosine


def middle_kernel(second_ref, third_ref, got_ref, back_ref, mid_ref):
    second_high, second_low = halves(second_ref[...])
    third_high, third_low = halves(third_ref[...])

    def apply(high, low, x):
        x_high, x_low = halves(x)
        return mul(high, x_high) + mul(low, x_high) + mul(high, x_low)

    @pl.loop(0, 16)
    def _(pair):
        sides = []
        for side in range(2):
            column = pair * 2 + side
            start = (column // 4) * 32 + column % 4
            sides.append(
                jnp.concatenate(
                    [
                        got_ref[pl.ds(start + part * 16 + inner * 4, 32, stride=256), :]
                        for part in range(2)
                        for inner in range(4)
                    ],
                    axis=0,
                )
            )
        out = apply(second_high, second_low, jnp.concatenate(sides, axis=1))
        for side in range(2):
            column = pair * 2 + side
            for part in range(2):
                rows = pl.ds(pl.multiple_of(part * 4096 + column * GATE, GATE), GATE)
                mid_ref[rows, :] = out[part * GATE : (part + 1) * GATE, side * GATE : (side + 1) * GATE]

    @pl.loop(0, 16)
    def _(pair):
        sides = []
        for side in range(2):
            sides.append(
                jnp.concatenate(
                    [
                        mid_ref[pl.ds(part * 4096 + pair * 2 + side, GATE, stride=32), :]
                        for part in range(2)
                    ],
                    axis=0,
                )
            )
        out = apply(third_high, third_low, jnp.concatenate(sides, axis=1))
        for side in range(2):
            rows = pl.ds(pl.multiple_of((pair * 2 + side) * 256, 256), 256)
            back_ref[rows, :] = out[:, side * GATE : (side + 1) * GATE]


def last_kernel(got_ref, real_ref, imag_ref):
    devices = real_ref.shape[0] // 16
    for part, ref in enumerate((real_ref, imag_ref)):

        @pl.loop(0, 16)
        def _(top):
            rows = pl.ds(pl.multiple_of(top * devices, devices), devices)
            ref[rows, :] = got_ref[pl.ds(top + part * 16, devices, stride=32), :]


def ordered(gate_pair, order_row, row_states, column_states):
    def one_hot(states):
        places = jnp.arange(QUBITS, dtype=jnp.int32)
        digits = states[:, None] >> places[None, :] & 1
        mapped = jnp.sum(digits << order_row[None, :], axis=1)
        return (mapped[:, None] == jnp.arange(GATE, dtype=jnp.int32)[None, :]).astype(f32)

    precise = lax.Precision.HIGHEST
    left, right = one_hot(row_states), one_hot(column_states)
    return [
        jnp.dot(jnp.dot(left, part, precision=precise), right.T, precision=precise)
        for part in (gate_pair[0], gate_pair[1])
    ]


def body(state_real, state_imag, gates, gate_orders, phase_masks, phase_angles):
    real_part = state_real[0, 0]
    imag_part = state_imag[0, 0]
    rows, columns = real_part.shape
    wide_count = lax.axis_size("wide")
    narrow_count = lax.axis_size("narrow")
    devices = wide_count * narrow_count
    base = (lax.axis_index("narrow") * wide_count + lax.axis_index("wide")) * (rows * columns)
    packed = jax.ShapeDtypeStruct((devices * 32, columns), f32)
    send = pl.pallas_call(
        front_kernel,
        out_shape=packed,
        in_specs=[SMEM] * 4 + [VMEM] * 3,
        out_specs=VMEM,
        scratch_shapes=[pltpu.VMEM((256, 256), bf16), pltpu.VMEM((256, 256), bf16)],
        name="front",
    )(base[None], gate_orders, phase_masks, phase_angles, real_part, imag_part, gates)

    def exchange(block):
        return lax.all_to_all(
            block.reshape(devices, 2, 16, columns), AXES, split_axis=0, concat_axis=0, tiled=True
        ).reshape(devices * 32, columns)

    got = exchange(send)
    states = jnp.arange(GATE, dtype=jnp.int32)
    by_inner = states % 32 * 4 + states // 32
    second = ordered(gates[1], gate_orders[1], by_inner, by_inner)
    swapped = states // 16 * 16 + states % 4 * 4 + states // 4 % 4
    third = ordered(gates[2], gate_orders[2], states, swapped)
    second = jnp.concatenate(
        [
            jnp.concatenate([second[0], -second[1]], axis=1),
            jnp.concatenate([second[1], second[0]], axis=1),
        ],
        axis=0,
    )
    third = jnp.stack(
        [
            jnp.concatenate([third[0], -third[1]], axis=1).reshape(8, 16, 256),
            jnp.concatenate([third[1], third[0]], axis=1).reshape(8, 16, 256),
        ],
        axis=1,
    ).reshape(256, 256)
    back = pl.pallas_call(
        middle_kernel,
        out_shape=packed,
        in_specs=[VMEM] * 3,
        out_specs=VMEM,
        scratch_shapes=[pltpu.VMEM((8192, GATE), f32)],
        name="middle",
    )(second, third, got)
    final = exchange(back)
    part = jax.ShapeDtypeStruct((rows, columns), f32)
    out_real, out_imag = pl.pallas_call(
        last_kernel,
        out_shape=(part, part),
        in_specs=[VMEM],
        out_specs=(VMEM, VMEM),
        name="last",
    )(final)
    return (out_real[None, None], out_imag[None, None])


def solution(mesh):
    placed = (P("narrow", "wide", None, None), P("narrow", "wide", None, None), P(), P(), P(), P())
    return jax.shard_map(
        body,
        mesh=mesh,
        in_specs=placed,
        out_specs=(P("narrow", "wide", None, None), P("narrow", "wide", None, None)),
        check_vma=False,
    )
```

```python
import jax
import jax.numpy as jnp
from jax import lax
from jax.experimental import pallas as pl
from jax.experimental.pallas import tpu as pltpu
from jax.sharding import Mesh
from jax.sharding import PartitionSpec as P


PLANE = ("x", "c", "y")
DEPTH = ("zh", "zl")
QUBITS = 7
GATE = 128
f32 = jnp.float32
bf16 = jnp.bfloat16
VMEM = pl.BlockSpec(memory_space=pltpu.VMEM)
SMEM = pl.BlockSpec(memory_space=pltpu.SMEM)


def halves(value):
    high = value.astype(bf16)
    return high, (value - high.astype(f32)).astype(bf16)


def mul(left, right):
    return jnp.dot(left, right, preferred_element_type=f32)


def pick(states, orders_ref, row):
    mapped = jnp.zeros_like(states)
    for place in range(QUBITS):
        mapped = mapped + (((states >> place) & 1) << orders_ref[row, place])
    return (mapped == lax.broadcasted_iota(jnp.int32, (GATE, GATE), 1)).astype(bf16)


def chosen(left, right, gate):
    out = []
    for part in halves(gate):
        rows = mul(left, part).astype(bf16)
        out.append(
            lax.dot_general(rows, right, (((1,), (1,)), ((), ())), preferred_element_type=f32)
            .astype(bf16)
        )
    return out


def sincos(angle):
    turns = jnp.floor(angle * 0.6366197723675814 + 0.5)
    r = angle - turns * 1.5703125
    r = r - turns * 4.8351287841796875e-4
    r = r - turns * 3.13855707645416e-7
    s = r * r
    sine = r + r * s * (-1.6666654611e-1 + s * (8.3321608736e-3 - s * 1.9515295891e-4))
    cosine = 1.0 - 0.5 * s + s * s * (
        4.166664568298827e-2 + s * (-1.388731625493765e-3 + s * 2.443315711809948e-5)
    )
    quarter = turns.astype(jnp.int32)
    swap = (quarter & 1) == 1
    base_sin = jnp.where(swap, cosine, sine)
    base_cos = jnp.where(swap, sine, cosine)
    sine = jnp.where((quarter & 2) == 2, -base_sin, base_sin)
    cosine = jnp.where(((quarter + 1) & 2) == 2, -base_cos, base_cos)
    return sine, cosine


def front_kernel(
    base_ref, me_ref, orders_ref, masks_ref, angles_ref, real_ref, imag_ref, gates_ref, *rest
):
    slab_refs, flat_ref, high_ref, low_ref, depth_ref = rest[:8], rest[8], rest[9], rest[10], rest[11]
    states = lax.broadcasted_iota(jnp.int32, (GATE, GATE), 0)
    one_hot = pick(states, orders_ref, 0)
    real_high, real_low = chosen(one_hot, one_hot, gates_ref[0, 0])
    imag_high, imag_low = chosen(one_hot, one_hot, gates_ref[0, 1])
    for ref, real, imag in ((high_ref, real_high, imag_high), (low_ref, real_low, imag_low)):
        ref[:GATE, :GATE] = real
        ref[:GATE, GATE:] = -imag
        ref[GATE:, :GATE] = imag
        ref[GATE:, GATE:] = real

    def turned(left, right):
        return lax.dot_general(left, right, (((1,), (1,)), ((), ())), preferred_element_type=f32)

    shape = (256, GATE)
    lane = lax.broadcasted_iota(jnp.int32, shape, 1)
    within = lax.broadcasted_iota(jnp.int32, shape, 0) * GATE + lane
    lower = lane < 64

    @pl.loop(0, 16)
    def _(top):
        rows = pl.ds(pl.multiple_of(top * 256, 256), 256)
        both = jnp.concatenate([real_ref[rows, :], imag_ref[rows, :]], axis=1)
        x_high, x_low = halves(both)
        new = (
            turned(x_high, high_ref[...])
            + turned(x_high, low_ref[...])
            + turned(x_low, high_ref[...])
        )
        flat = within + (base_ref[0] + top * (256 * GATE))
        angle = jnp.zeros(shape, f32)
        for pair in range(masks_ref.shape[0]):
            mask = masks_ref[pair, 0] | masks_ref[pair, 1]
            angle = angle + jnp.where((flat & mask) == mask, angles_ref[pair], 0.0)
        sine, cosine = sincos(angle)
        real = new[:, :GATE]
        imag = new[:, GATE:]
        real, imag = real * cosine - imag * sine, real * sine + imag * cosine
        depth_ref[pl.ds(top, 256, stride=16), :] = jnp.where(lower, real, pltpu.roll(imag, 64, 1))
        flat_ref[pl.ds(top, 256, stride=16), :] = jnp.where(lower, pltpu.roll(real, 64, 1), imag)

    spread(depth_ref, me_ref, slab_refs)


def spread(depth_ref, me_ref, slab_refs):
    for shift, ref in enumerate(slab_refs):
        start = ((me_ref[0] + shift) & 7) * 512
        ref[...] = depth_ref[pl.ds(pl.multiple_of(start, 512), 512), :]


def gather_in(slab_refs, me_ref, depth_ref):
    for shift, ref in enumerate(slab_refs):
        start = ((me_ref[0] - shift) & 7) * 512
        depth_ref[pl.ds(pl.multiple_of(start, 512), 512), :] = ref[...]


def apply_gates(second_ref, third_ref, got_ref, back_ref, mid_ref, depth, plane):
    second_high, second_low = halves(second_ref[...])
    third_high, third_low = halves(third_ref[...])
    lower = lax.broadcasted_iota(jnp.int32, (GATE, GATE), 1) < 64

    def with_turned(x):
        other = pltpu.roll(x, 64, 1)
        return jnp.concatenate([x, jnp.where(lower, -other, other)], axis=0)

    def apply(high, low, x):
        x_high, x_low = halves(x)
        return mul(high, x_high) + mul(low, x_high) + mul(high, x_low)

    @pl.loop(0, 16)
    def _(pair):
        sides = []
        for side in range(2):
            column = pair * 2 + side
            start = (column // 8) * plane + (column // 4 % 2) * depth + column % 4
            sides.append(
                with_turned(
                    jnp.concatenate(
                        [
                            got_ref[pl.ds(start + zh * 2 * depth + inner * 4, 8, stride=4 * plane), :]
                            for inner in range(4)
                            for zh in range(4)
                        ],
                        axis=0,
                    )
                )
            )
        out = apply(second_high, second_low, jnp.concatenate(sides, axis=1))
        for side in range(2):
            rows = pl.ds(pl.multiple_of((pair * 2 + side) * GATE, GATE), GATE)
            mid_ref[rows, :] = out[:, side * GATE : (side + 1) * GATE]

    @pl.loop(0, 16)
    def _(pair):
        sides = [
            with_turned(mid_ref[pl.ds(pair * 2 + side, GATE, stride=32), :]) for side in range(2)
        ]
        out = apply(third_high, third_low, jnp.concatenate(sides, axis=1))
        for side in range(2):
            wide = pair * 2 + side
            start = (wide // 8) * 2 * depth + (wide % 8) * 4 * plane
            for narrow in range(8):
                rows = pl.ds(
                    pl.multiple_of(start + narrow // 2 * plane + narrow % 2 * depth, 16), 16
                )
                back_ref[rows, :] = out[
                    narrow * 16 : (narrow + 1) * 16, side * GATE : (side + 1) * GATE
                ]


def flat_kernel(second_ref, third_ref, got_ref, back_ref, mid_ref):
    apply_gates(second_ref, third_ref, got_ref, back_ref, mid_ref, 16, 128)


def depth_kernel(me_ref, second_ref, third_ref, *rest):
    slab_refs, back_refs, depth_ref, mid_ref = rest[:8], rest[8:16], rest[16], rest[17]
    gather_in(slab_refs, me_ref, depth_ref)
    apply_gates(second_ref, third_ref, depth_ref, depth_ref, mid_ref, 512, 16)
    spread(depth_ref, me_ref, back_refs)


def split_kernel(me_ref, flat_ref, *slab_refs):
    for shift, ref in enumerate(slab_refs):
        ref[...] = flat_ref[:, (me_ref[0] + shift) & 7]


def join_kernel(me_ref, *refs):
    for shift, ref in enumerate(refs[:8]):
        refs[8][:, (me_ref[0] - shift) & 7] = ref[...]


def last_kernel(me_ref, *rest):
    slab_refs, flat_ref, real_ref, imag_ref, depth_ref = rest[:8], rest[8], rest[9], rest[10], rest[11]
    gather_in(slab_refs, me_ref, depth_ref)
    lower = lax.broadcasted_iota(jnp.int32, (256, GATE), 1) < 64

    @pl.loop(0, 16)
    def _(top):
        rows = pl.ds(pl.multiple_of(top * 256, 256), 256)
        first = depth_ref[pl.ds(top, 256, stride=16), :]
        second = flat_ref[pl.ds(top, 256, stride=16), :]
        real_ref[rows, :] = jnp.where(lower, first, pltpu.roll(second, 64, 1))
        imag_ref[rows, :] = jnp.where(lower, pltpu.roll(first, 64, 1), second)


def ordered(gate_pair, order_row, row_states, column_states):
    def one_hot(states):
        places = jnp.arange(QUBITS, dtype=jnp.int32)
        digits = states[:, None] >> places[None, :] & 1
        mapped = jnp.sum(digits << order_row[None, :], axis=1)
        return (mapped[:, None] == jnp.arange(GATE, dtype=jnp.int32)[None, :]).astype(f32)

    precise = lax.Precision.HIGHEST
    left, right = one_hot(row_states), one_hot(column_states)
    return [
        jnp.dot(jnp.dot(left, part, precision=precise), right.T, precision=precise)
        for part in (gate_pair[0], gate_pair[1])
    ]


def body(state_real, state_imag, gates, gate_orders, phase_masks, phase_angles):
    real_part = state_real[0, 0]
    imag_part = state_imag[0, 0]
    rows, columns = real_part.shape
    wide = ("x", "zh", "c")
    narrow = ("y", "zl")
    base = (lax.axis_index(narrow) * lax.axis_size(wide) + lax.axis_index(wide)) * (rows * columns)
    me = lax.axis_index(DEPTH)[None]
    whole = jax.ShapeDtypeStruct((rows, columns), f32)
    grouped = jax.ShapeDtypeStruct((32, 8, 16, columns), f32)
    slab = jax.ShapeDtypeStruct((512, columns), f32)
    block = jax.ShapeDtypeStruct((32, 16, columns), f32)
    room = pltpu.VMEM((rows, columns), f32)

    def call(kernel, out_shape, scalars, arrays, scratch=(), work=1, after=()):
        outs = (VMEM,) * len(out_shape) if isinstance(out_shape, tuple) else VMEM
        first = len(scalars) + len(arrays)

        def run(*refs):
            kernel(*refs[:first], *refs[first + len(after) :])

        return pl.pallas_call(
            run,
            out_shape=out_shape,
            in_specs=[SMEM] * len(scalars)
            + [VMEM] * len(arrays)
            + [pl.BlockSpec(memory_space=pl.ANY)] * len(after),
            out_specs=outs,
            scratch_shapes=list(scratch),
            cost_estimate=pl.CostEstimate(
                flops=work * 10**9, bytes_accessed=work * 4 * 2**20, transcendentals=0
            ),
        )(*scalars, *arrays, *after)

    def along(slabs):
        moved = [slabs[0]]
        for shift in range(1, 8):
            route = [(z, (z + shift) % 8) for z in range(8)]
            moved.append(lax.ppermute(slabs[shift], DEPTH, route))
        return moved

    def across(array):
        return lax.all_to_all(
            array.reshape(32, 128, columns), PLANE, split_axis=0, concat_axis=0, tiled=True
        )

    *slabs, flat = call(
        front_kernel,
        (slab,) * 8 + (whole,),
        [base[None], me, gate_orders, phase_masks, phase_angles],
        [real_part, imag_part, gates],
        [pltpu.VMEM((256, 256), bf16), pltpu.VMEM((256, 256), bf16), room],
        work=3,
    )
    states = jnp.arange(GATE, dtype=jnp.int32)
    zh, xc = states // 8 % 4, states % 8
    inner = states // 32
    column_states = ((xc // 2 * 8) + zh * 2 + xc % 2) * 4 + inner
    spot = states % 32
    row_states = (spot % 8 // 2 * 8 + spot // 8 * 2 + spot % 2) * 4 + inner
    second = jnp.concatenate(ordered(gates[1], gate_orders[1], row_states, column_states), axis=1)
    swapped = states // 16 * 16 + states % 4 * 4 + states // 4 % 4
    third = jnp.concatenate(ordered(gates[2], gate_orders[2], states, swapped), axis=1)

    slabs = along(slabs)
    flat = across(flat)
    pieces = call(split_kernel, (block,) * 8, [me], [flat.reshape(32, 8, 16, columns)])
    last_sent = pieces[7]
    pieces = along([piece.reshape(512, columns) for piece in pieces])
    slabs = [piece.reshape(32, 16, columns) for piece in slabs]
    joined = call(join_kernel, grouped, [me], slabs, after=[last_sent])
    joined = across(joined).reshape(rows, columns)
    joined = call(flat_kernel, whole, [], [second, third, joined], [room], work=2)
    pieces = call(
        depth_kernel,
        (slab,) * 8,
        [me],
        [second, third, *pieces],
        [room, room],
        work=2,
        after=[joined],
    )
    pieces = along(pieces)
    joined = across(joined)
    slabs = call(split_kernel, (block,) * 8, [me], [joined.reshape(32, 8, 16, columns)])
    last_sent = slabs[7]
    slabs = along([piece.reshape(512, columns) for piece in slabs])
    pieces = [piece.reshape(32, 16, columns) for piece in pieces]
    flat = call(join_kernel, grouped, [me], pieces, after=[last_sent])
    flat = across(flat).reshape(rows, columns)
    out_real, out_imag = call(last_kernel, (whole, whole), [me], [*slabs, flat], [room], work=2)
    return (out_real[None, None], out_imag[None, None])


def solution(mesh):
    fine = Mesh(mesh.devices.reshape(4, 4, 2, 4, 2), ("x", "zh", "c", "y", "zl"))
    state = P(("y", "zl"), ("x", "zh", "c"), None, None)
    return jax.shard_map(
        body,
        mesh=fine,
        in_specs=(state, state, P(), P(), P(), P()),
        out_specs=(state, state),
        check_vma=False,
    )
```

```python
import functools

import jax
import jax.numpy as jnp
from jax import lax
from jax.experimental import pallas as pl
from jax.experimental.pallas import tpu as pltpu
from jax.sharding import PartitionSpec as P

AXES = ("wide", "narrow")
QUBITS = 7
FRONT_ROWS = 64
LAST_ROWS = 64
GATE = 128
f32 = jnp.float32
bf16 = jnp.bfloat16
VMEM = pl.BlockSpec(memory_space=pltpu.VMEM)
SMEM = pl.BlockSpec(memory_space=pltpu.SMEM)


def halves(value):
    high = value.astype(bf16)
    return high, (value - high.astype(f32)).astype(bf16)


def mul(left, right):
    return jnp.dot(left, right, preferred_element_type=f32)


def pick(states, orders_ref, row):
    mapped = jnp.zeros_like(states)
    for place in range(QUBITS):
        mapped = mapped + (((states >> place) & 1) << orders_ref[row, place])
    return (mapped == lax.broadcasted_iota(jnp.int32, (GATE, GATE), 1)).astype(bf16)


def chosen(left, right, gate):
    out = []
    for part in halves(gate):
        rows = mul(left, part).astype(bf16)
        out.append(
            lax.dot_general(rows, right, (((1,), (1,)), ((), ())), preferred_element_type=f32)
            .astype(bf16)
        )
    return out


def unit_turn(quarters):
    whole = jnp.floor(quarters + 0.5)
    r = (quarters - whole) * 1.5707963267948966
    s = r * r
    sine = r + r * s * (-1.6666654611e-1 + s * (8.3321608736e-3 - s * 1.9515295891e-4))
    cosine = 1.0 - 0.5 * s + s * s * (
        4.166664568298827e-2 + s * (-1.388731625493765e-3 + s * 2.443315711809948e-5)
    )
    quarter = whole.astype(jnp.int32)
    swap = (quarter & 1) == 1
    base_sin = jnp.where(swap, cosine, sine)
    base_cos = jnp.where(swap, sine, cosine)
    sine = jnp.where((quarter & 2) == 2, -base_sin, base_sin)
    cosine = jnp.where(((quarter + 1) & 2) == 2, -base_cos, base_cos)
    return cosine, sine


def front_kernel(base_ref, orders_ref, masks_ref, angles_ref, real_ref, imag_ref, gates_ref,
                 send_ref, high_ref, low_ref, need_ref, angle_ref):
    top, count = real_ref.shape[:2]
    pairs = masks_ref.shape[0]
    step = pl.program_id(0)

    @pl.when(step == 0)
    def _():
        states = lax.broadcasted_iota(jnp.int32, (GATE, GATE), 0)
        one_hot = pick(states, orders_ref, 0)
        real_high, real_low = chosen(one_hot, one_hot, gates_ref[0, 0])
        imag_high, imag_low = chosen(one_hot, one_hot, gates_ref[0, 1])
        for ref, real, imag in ((high_ref, real_high, imag_high), (low_ref, real_low, imag_low)):
            ref[:GATE, :GATE] = real
            ref[:GATE, GATE:] = -imag
            ref[GATE:, :GATE] = imag
            ref[GATE:, GATE:] = real
        lane = lax.broadcasted_iota(jnp.int32, (8, GATE), 1)
        column = lax.broadcasted_iota(jnp.int32, (GATE, GATE), 1)
        row = lax.broadcasted_iota(jnp.int32, (GATE, GATE), 0)
        need = jnp.zeros((8, GATE), jnp.int32) - 1
        values = jnp.zeros((GATE, GATE), f32)
        for pair in range(pairs):
            mask = masks_ref[pair, 0] | masks_ref[pair, 1]
            inside = mask & (GATE - 1)
            quarters = jnp.full((GATE, GATE), angles_ref[pair] * 0.6366197723675814, f32)
            held = jnp.where((column & inside) == inside, quarters, 0.0)
            for part in range(3):
                spot = part * pairs + pair
                need = jnp.where(lane == spot, mask & ~(GATE - 1), need)
                piece = held.astype(bf16).astype(f32)
                values = jnp.where(row == spot, piece, values)
                held = held - piece
        need_ref[...] = need
        angle_ref[...] = values.astype(bf16)

    def turned(left, right):
        return lax.dot_general(left, right, (((1,), (1,)), ((), ())), preferred_element_type=f32)

    rows = top * count
    both = jnp.concatenate(
        [real_ref[...].reshape(rows, GATE), imag_ref[...].reshape(rows, GATE)], axis=1
    )
    x_high, x_low = halves(both)
    new = (
        turned(x_high, high_ref[...])
        + turned(x_high, low_ref[...])
        + turned(x_low, high_ref[...])
    )
    shape = (top, count, GATE)
    flat = (
        lax.broadcasted_iota(jnp.int32, shape, 0) * (256 * GATE)
        + lax.broadcasted_iota(jnp.int32, shape, 1) * GATE
        + (base_ref[0] + step * (count * GATE))
    ).reshape(rows, GATE)
    need = need_ref[0:1, :]
    conditions = jnp.where((flat & need) == need, 1.0, 0.0).astype(bf16)
    cosine, sine = unit_turn(mul(conditions, angle_ref[...]))
    real = new[:, :GATE]
    imag = new[:, GATE:]
    for part, value in enumerate((real * cosine - imag * sine, real * sine + imag * cosine)):
        send_ref[:, part] = jnp.transpose(value.reshape(shape), (1, 0, 2))


def middle_kernel(second_ref, third_ref, got_ref, back_ref, mid_ref, high_ref, low_ref):
    step = pl.program_id(0)
    inputs = got_ref.shape[0]

    @pl.when(step == 0)
    def _():
        high_ref[0], low_ref[0] = halves(second_ref[...])
        high_ref[1], low_ref[1] = halves(third_ref[...])

    def apply(which, x):
        x_high, x_low = halves(x)
        high = high_ref[which]
        return mul(high, x_high) + mul(low_ref[which], x_high) + mul(high, x_low)

    @pl.when(step < 8)
    def _():
        parts = [jnp.transpose(got_ref[:, 0, part], (1, 0, 2)) for part in range(2)]
        columns = [
            jnp.concatenate([part[inner * 4 + rest] for part in parts for inner in range(4)], axis=0)
            for rest in range(4)
        ]
        out = apply(0, jnp.concatenate(columns, axis=1))
        for part in range(2):
            stack = jnp.stack(
                [
                    out[
                        part * GATE + inner * inputs : part * GATE + (inner + 1) * inputs,
                        rest * GATE : (rest + 1) * GATE,
                    ]
                    for rest in range(4)
                    for inner in range(4)
                ],
                axis=0,
            )
            mid_ref[part, :, step] = jnp.transpose(stack, (1, 0, 2))

    @pl.when(step >= 8)
    def _():
        count = back_ref.shape[0]
        first = (step - 8) * count
        columns = [
            jnp.concatenate(
                [mid_ref[part, first + wide].reshape(GATE, GATE) for part in range(2)], axis=0
            )
            for wide in range(count)
        ]
        out = apply(1, jnp.concatenate(columns, axis=1))
        for wide in range(count):
            back_ref[wide] = out[:, wide * GATE : (wide + 1) * GATE].reshape(8, 2, 16, GATE)


def last_kernel(got_ref, real_ref, imag_ref):
    for part, ref in enumerate((real_ref, imag_ref)):
        ref[...] = jnp.transpose(got_ref[:, part], (1, 0, 2))


def ordered(gate_pair, order_row, row_states, column_states):
    def one_hot(states):
        places = jnp.arange(QUBITS, dtype=jnp.int32)
        digits = states[:, None] >> places[None, :] & 1
        mapped = jnp.sum(digits << order_row[None, :], axis=1)
        return (mapped[:, None] == jnp.arange(GATE, dtype=jnp.int32)[None, :]).astype(f32)

    precise = lax.Precision.HIGHEST
    left, right = one_hot(row_states), one_hot(column_states)
    return [
        jnp.dot(jnp.dot(left, part, precision=precise), right.T, precision=precise)
        for part in (gate_pair[0], gate_pair[1])
    ]


def body(state_real, state_imag, gates, gate_orders, phase_masks, phase_angles):
    real_part = state_real[0, 0]
    imag_part = state_imag[0, 0]
    rows, columns = real_part.shape
    wide_count = lax.axis_size("wide")
    narrow_count = lax.axis_size("narrow")
    devices = wide_count * narrow_count
    base = (lax.axis_index("narrow") * wide_count + lax.axis_index("wide")) * (rows * columns)
    packed = jax.ShapeDtypeStruct((devices, 2, 16, columns), f32)
    tall = jax.ShapeDtypeStruct((16, devices, columns), f32)
    count = FRONT_ROWS
    piece = pl.BlockSpec((16, count, columns), lambda i: (0, i, 0))
    send = pl.pallas_call(
        front_kernel,
        out_shape=packed,
        grid=(devices // count,),
        in_specs=[SMEM] * 4 + [piece, piece, VMEM],
        out_specs=pl.BlockSpec((count, 2, 16, columns), lambda i: (i, 0, 0, 0)),
        scratch_shapes=[
            pltpu.VMEM((256, 256), bf16),
            pltpu.VMEM((256, 256), bf16),
            pltpu.VMEM((8, GATE), jnp.int32),
            pltpu.VMEM((GATE, GATE), bf16),
        ],
        name="front",
    )(
        base[None],
        gate_orders,
        phase_masks,
        phase_angles,
        real_part.reshape(16, devices, columns),
        imag_part.reshape(16, devices, columns),
        gates,
    )

    def exchange(block):
        return lax.all_to_all(block, AXES, split_axis=0, concat_axis=0, tiled=True)

    got = exchange(send)
    states = jnp.arange(GATE, dtype=jnp.int32)
    by_inner = states % 32 * 4 + states // 32
    second = ordered(gates[1], gate_orders[1], by_inner, by_inner)
    swapped = states // 16 * 16 + states % 4 * 4 + states // 4 % 4
    third = ordered(gates[2], gate_orders[2], states, swapped)
    second = jnp.concatenate(
        [
            jnp.concatenate([second[0], -second[1]], axis=1),
            jnp.concatenate([second[1], second[0]], axis=1),
        ],
        axis=0,
    )
    third = jnp.stack(
        [
            jnp.concatenate([third[0], -third[1]], axis=1).reshape(8, 16, 256),
            jnp.concatenate([third[1], third[0]], axis=1).reshape(8, 16, 256),
        ],
        axis=1,
    ).reshape(256, 256)
    back = pl.pallas_call(
        middle_kernel,
        out_shape=jax.ShapeDtypeStruct((wide_count, narrow_count, 2, 16, columns), f32),
        grid=(16,),
        in_specs=[
            VMEM,
            VMEM,
            pl.BlockSpec(
                (wide_count, 1, 2, 16, columns), lambda i: (0, jnp.minimum(i, 7), 0, 0, 0)
            ),
        ],
        out_specs=pl.BlockSpec(
            (wide_count // 8, narrow_count, 2, 16, columns),
            lambda i: (jnp.maximum(i - 8, 0), 0, 0, 0, 0),
        ),
        scratch_shapes=[
            pltpu.VMEM((2, wide_count, narrow_count, 16, columns), f32),
            pltpu.VMEM((2, 256, 256), bf16),
            pltpu.VMEM((2, 256, 256), bf16),
        ],
        name="middle",
    )(second, third, got.reshape(wide_count, narrow_count, 2, 16, columns))
    final = exchange(back.reshape(devices, 2, 16, columns))
    count = LAST_ROWS
    piece = pl.BlockSpec((16, count, columns), lambda i: (0, i, 0))
    out_real, out_imag = pl.pallas_call(
        last_kernel,
        out_shape=(tall, tall),
        grid=(devices // count,),
        in_specs=[pl.BlockSpec((count, 2, 16, columns), lambda i: (i, 0, 0, 0))],
        out_specs=(piece, piece),
        name="last",
    )(final)
    out_real, out_imag = out_real.reshape(rows, columns), out_imag.reshape(rows, columns)
    return (out_real[None, None], out_imag[None, None])


def solution(mesh):
    placed = (P("narrow", "wide", None, None), P("narrow", "wide", None, None), P(), P(), P(), P())
    return jax.shard_map(
        body,
        mesh=mesh,
        in_specs=placed,
        out_specs=(P("narrow", "wide", None, None), P("narrow", "wide", None, None)),
        check_vma=False,
    )
```

```python
import functools

import jax
import jax.numpy as jnp
from jax import lax
from jax.experimental import pallas as pl
from jax.experimental.pallas import tpu as pltpu
from jax.sharding import PartitionSpec as P

AXES = ("wide", "narrow")
QUBITS = 7
FRONT_ROWS = 64
LAST_ROWS = 128
GATE_STEPS = 2
GATE = 128
f32 = jnp.float32
bf16 = jnp.bfloat16
VMEM = pl.BlockSpec(memory_space=pltpu.VMEM)
SMEM = pl.BlockSpec(memory_space=pltpu.SMEM)


def halves(value):
    high = value.astype(bf16)
    return high, (value - high.astype(f32)).astype(bf16)


def mul(left, right):
    return jnp.dot(left, right, preferred_element_type=f32)


def pick(states, orders_ref, row):
    mapped = jnp.zeros_like(states)
    for place in range(QUBITS):
        mapped = mapped + (((states >> place) & 1) << orders_ref[row, place])
    return (mapped == lax.broadcasted_iota(jnp.int32, (GATE, GATE), 1)).astype(bf16)


def chosen(left, right, gate):
    out = []
    for part in halves(gate):
        rows = mul(left, part).astype(bf16)
        out.append(
            lax.dot_general(rows, right, (((1,), (1,)), ((), ())), preferred_element_type=f32)
            .astype(bf16)
        )
    return out


def unit_turn(quarters):
    whole = jnp.floor(quarters + 0.5)
    r = (quarters - whole) * 1.5707963267948966
    s = r * r
    sine = r + r * s * (-1.6666654611e-1 + s * (8.3321608736e-3 - s * 1.9515295891e-4))
    cosine = 1.0 - 0.5 * s + s * s * (
        4.166664568298827e-2 + s * (-1.388731625493765e-3 + s * 2.443315711809948e-5)
    )
    quarter = whole.astype(jnp.int32)
    swap = (quarter & 1) == 1
    base_sin = jnp.where(swap, cosine, sine)
    base_cos = jnp.where(swap, sine, cosine)
    sine = jnp.where((quarter & 2) == 2, -base_sin, base_sin)
    cosine = jnp.where(((quarter + 1) & 2) == 2, -base_cos, base_cos)
    return cosine, sine


def front_kernel(base_ref, orders_ref, masks_ref, angles_ref, real_ref, imag_ref, gates_ref,
                 send_ref, gate_ref, need_ref, weight_ref, table_ref, place_ref):
    top, count = real_ref.shape[:2]
    pairs = masks_ref.shape[1]
    patterns = 2**pairs
    rows = top * count
    step = pl.program_id(0)
    order = range(top)

    @pl.when(step == 0)
    def _():
        states = lax.broadcasted_iota(jnp.int32, (GATE, GATE), 0)
        one_hot = pick(states, orders_ref, 0)
        real_high, real_low = chosen(one_hot, one_hot, gates_ref[0, 0])
        imag_high, imag_low = chosen(one_hot, one_hot, gates_ref[0, 1])
        for spot, real, imag in (
            (0, real_high, imag_high),
            (2, real_low, imag_low),
            (4, real_high, imag_high),
        ):
            left = slice(spot * GATE, (spot + 1) * GATE)
            right = slice((spot + 1) * GATE, (spot + 2) * GATE)
            gate_ref[:GATE, left] = real
            gate_ref[:GATE, right] = -imag
            gate_ref[GATE:, left] = imag
            gate_ref[GATE:, right] = real
        lane = lax.broadcasted_iota(jnp.int32, (8, GATE), 1)
        spot = lax.broadcasted_iota(jnp.int32, (GATE, GATE), 0)
        column = lax.broadcasted_iota(jnp.int32, (patterns, GATE), 1)
        pattern = lax.broadcasted_iota(jnp.int32, (patterns, GATE), 0)
        need = jnp.zeros((8, GATE), jnp.int32) - 1
        weight = jnp.zeros((GATE, GATE), f32)
        quarters = jnp.zeros((patterns, GATE), f32)
        for pair in range(pairs):
            mask = masks_ref[0, pair] | masks_ref[1, pair]
            inside = mask & (GATE - 1)
            need = jnp.where(lane == pair, mask & ~(GATE - 1), need)
            weight = jnp.where(spot == pair, float(2**pair), weight)
            met = ((column & inside) == inside) & (((pattern >> pair) & 1) == 1)
            quarters = quarters + jnp.where(met, angles_ref[pair] * 0.6366197723675814, 0.0)
        need_ref[...] = need
        weight_ref[...] = weight.astype(bf16)
        for half, value in enumerate(unit_turn(quarters)):
            lanes = slice(half * GATE, (half + 1) * GATE)
            table_ref[:patterns, lanes], table_ref[patterns:, lanes] = halves(value)
        within = lax.broadcasted_iota(jnp.int32, (count, GATE), 0) * GATE
        for spot, high in enumerate(order):
            place_ref[spot] = within + (base_ref[0] + high * (256 * GATE))

    both = jnp.concatenate(
        [
            jnp.concatenate([ref[high] for high in order], axis=0)
            for ref in (real_ref, imag_ref)
        ],
        axis=1,
    )
    x_high, x_low = halves(both)
    new = lax.dot_general(
        jnp.concatenate([x_high, x_high, x_low], axis=1),
        gate_ref[...],
        (((1,), (1,)), ((), ())),
        preferred_element_type=f32,
    )
    flat = place_ref[...].reshape(rows, GATE) + step * (count * GATE)
    need = need_ref[0:1, :]
    conditions = jnp.where((flat & need) == need, 1.0, 0.0).astype(bf16)
    found = mul(conditions, weight_ref[...])
    lane = lax.broadcasted_iota(jnp.int32, (rows, GATE), 1).astype(f32)
    chosen_rows = [
        jnp.where(found == lane + float(first), 1.0, 0.0).astype(bf16)
        for first in range(0, patterns, GATE)
    ]
    turn = mul(jnp.concatenate(chosen_rows * 2, axis=1), table_ref[...])
    cosine, sine = turn[:, :GATE], turn[:, GATE:]
    real = new[:, :GATE]
    imag = new[:, GATE:]
    for part, value in enumerate((real * cosine - imag * sine, real * sine + imag * cosine)):
        send_ref[:, part] = jnp.transpose(value.reshape(top, count, GATE), (1, 0, 2))


def middle_kernel(second_ref, third_ref, got_ref, back_ref, mid_ref, gates_ref):
    step = pl.program_id(0)
    inputs, together = got_ref.shape[:2]
    steps = 8 // together

    @pl.when(step == 0)
    def _():
        for which, ref in enumerate((second_ref, third_ref)):
            high, low = halves(ref[...])
            gates_ref[which] = jnp.concatenate([high, low, high], axis=1)

    def apply(which, x):
        x_high, x_low = halves(x)
        return mul(gates_ref[which], jnp.concatenate([x_high, x_high, x_low], axis=0))

    @pl.when(step < steps)
    def _():
        for narrow in range(together):
            parts = [jnp.transpose(got_ref[:, narrow, part], (1, 0, 2)) for part in range(2)]
            columns = [
                jnp.concatenate(
                    [part[inner * 4 + rest] for part in parts for inner in range(4)], axis=0
                )
                for rest in range(4)
            ]
            out = apply(0, jnp.concatenate(columns, axis=1))
            for part in range(2):
                stack = jnp.stack(
                    [
                        out[
                            part * GATE + inner * inputs : part * GATE + (inner + 1) * inputs,
                            rest * GATE : (rest + 1) * GATE,
                        ]
                        for rest in range(4)
                        for inner in range(4)
                    ],
                    axis=0,
                )
                mid_ref[part, :, step * together + narrow] = jnp.transpose(stack, (1, 0, 2))

    @pl.when(step >= steps)
    def _():
        count = back_ref.shape[0]

        for group in range(count // 4):
            first = (step - steps) * count + group * 4
            columns = [
                jnp.concatenate(
                    [mid_ref[part, first + wide].reshape(GATE, GATE) for part in range(2)], axis=0
                )
                for wide in range(4)
            ]
            out = apply(1, jnp.concatenate(columns, axis=1))
            for wide in range(4):
                back_ref[group * 4 + wide] = out[:, wide * GATE : (wide + 1) * GATE].reshape(
                    8, 2, 16, GATE
                )


def last_kernel(got_ref, real_ref, imag_ref):
    for part, ref in enumerate((real_ref, imag_ref)):
        ref[...] = jnp.transpose(got_ref[:, part], (1, 0, 2))


def ordered(gate_pair, order_row, row_states, column_states):
    def one_hot(states):
        places = jnp.arange(QUBITS, dtype=jnp.int32)
        digits = states[:, None] >> places[None, :] & 1
        mapped = jnp.sum(digits << order_row[None, :], axis=1)
        return (mapped[:, None] == jnp.arange(GATE, dtype=jnp.int32)[None, :]).astype(f32)

    precise = lax.Precision.HIGHEST
    left, right = one_hot(row_states), one_hot(column_states)
    return [
        jnp.dot(jnp.dot(left, part, precision=precise), right.T, precision=precise)
        for part in (gate_pair[0], gate_pair[1])
    ]


def body(state_real, state_imag, gates, gate_orders, phase_masks, phase_angles):
    real_part = state_real[0, 0]
    imag_part = state_imag[0, 0]
    rows, columns = real_part.shape
    wide_count = lax.axis_size("wide")
    narrow_count = lax.axis_size("narrow")
    devices = wide_count * narrow_count
    base = (lax.axis_index("narrow") * wide_count + lax.axis_index("wide")) * (rows * columns)
    packed = jax.ShapeDtypeStruct((devices, 2, 16, columns), f32)
    tall = jax.ShapeDtypeStruct((16, devices, columns), f32)
    count = FRONT_ROWS
    piece = pl.BlockSpec((16, count, columns), lambda i: (0, i, 0))
    send = pl.pallas_call(
        front_kernel,
        out_shape=packed,
        grid=(devices // count,),
        in_specs=[SMEM] * 4 + [piece, piece, VMEM],
        out_specs=pl.BlockSpec((count, 2, 16, columns), lambda i: (i, 0, 0, 0)),
        scratch_shapes=[
            pltpu.VMEM((256, 768), bf16),
            pltpu.VMEM((8, GATE), jnp.int32),
            pltpu.VMEM((GATE, GATE), bf16),
            pltpu.VMEM((2 * 2 ** phase_masks.shape[0], 256), bf16),
            pltpu.VMEM((16, count, GATE), jnp.int32),
        ],
        name="front",
    )(
        base[None],
        gate_orders,
        phase_masks.T,
        phase_angles,
        real_part.reshape(16, devices, columns),
        imag_part.reshape(16, devices, columns),
        gates,
    )

    def exchange(block):
        return lax.all_to_all(block, AXES, split_axis=0, concat_axis=0, tiled=True)

    got = exchange(send)
    states = jnp.arange(GATE, dtype=jnp.int32)
    by_inner = states % 32 * 4 + states // 32
    second = ordered(gates[1], gate_orders[1], by_inner, by_inner)
    swapped = states // 16 * 16 + states % 4 * 4 + states // 4 % 4
    third = ordered(gates[2], gate_orders[2], states, swapped)
    second = jnp.concatenate(
        [
            jnp.concatenate([second[0], -second[1]], axis=1),
            jnp.concatenate([second[1], second[0]], axis=1),
        ],
        axis=0,
    )
    third = jnp.stack(
        [
            jnp.concatenate([third[0], -third[1]], axis=1).reshape(8, 16, 256),
            jnp.concatenate([third[1], third[0]], axis=1).reshape(8, 16, 256),
        ],
        axis=1,
    ).reshape(256, 256)
    back = pl.pallas_call(
        middle_kernel,
        out_shape=jax.ShapeDtypeStruct((wide_count, narrow_count, 2, 16, columns), f32),
        grid=(GATE_STEPS * 2,),
        in_specs=[
            VMEM,
            VMEM,
            pl.BlockSpec(
                (wide_count, narrow_count // GATE_STEPS, 2, 16, columns),
                lambda i: (0, jnp.minimum(i, GATE_STEPS - 1), 0, 0, 0),
            ),
        ],
        out_specs=pl.BlockSpec(
            (wide_count // GATE_STEPS, narrow_count, 2, 16, columns),
            lambda i: (jnp.maximum(i - GATE_STEPS, 0), 0, 0, 0, 0),
        ),
        scratch_shapes=[
            pltpu.VMEM((2, wide_count, narrow_count, 16, columns), f32),
            pltpu.VMEM((2, 256, 768), bf16),
        ],
        name="middle",
    )(second, third, got.reshape(wide_count, narrow_count, 2, 16, columns))
    final = exchange(back.reshape(devices, 2, 16, columns))
    count = LAST_ROWS
    piece = pl.BlockSpec((16, count, columns), lambda i: (0, i, 0))
    out_real, out_imag = pl.pallas_call(
        last_kernel,
        out_shape=(tall, tall),
        grid=(devices // count,),
        in_specs=[pl.BlockSpec((count, 2, 16, columns), lambda i: (i, 0, 0, 0))],
        out_specs=(piece, piece),
        name="last",
    )(final)
    out_real, out_imag = out_real.reshape(rows, columns), out_imag.reshape(rows, columns)
    return (out_real[None, None], out_imag[None, None])


def solution(mesh):
    placed = (P("narrow", "wide", None, None), P("narrow", "wide", None, None), P(), P(), P(), P())
    return jax.shard_map(
        body,
        mesh=mesh,
        in_specs=placed,
        out_specs=(P("narrow", "wide", None, None), P("narrow", "wide", None, None)),
        check_vma=False,
    )
```

```python
import functools

import jax
import jax.numpy as jnp
from jax import lax
from jax.experimental import pallas as pl
from jax.experimental.pallas import tpu as pltpu
from jax.sharding import PartitionSpec as P

AXES = ("wide", "narrow")
QUBITS = 7
FRONT_ROWS = 64
LAST_ROWS = 64
GATE_STEPS = 4
BACK_STEPS = 4
GATE = 128
f32 = jnp.float32
bf16 = jnp.bfloat16
VMEM = pl.BlockSpec(memory_space=pltpu.VMEM)
SMEM = pl.BlockSpec(memory_space=pltpu.SMEM)
ANY = pl.BlockSpec(memory_space=pl.ANY)
DMA = pltpu.SemaphoreType.DMA


def halves(value):
    high = value.astype(bf16)
    return high, (value - high.astype(f32)).astype(bf16)


def mul(left, right):
    return jnp.dot(left, right, preferred_element_type=f32)


def pick(states, orders_ref, row):
    mapped = jnp.zeros_like(states)
    for place in range(QUBITS):
        mapped = mapped + (((states >> place) & 1) << orders_ref[row, place])
    return (mapped == lax.broadcasted_iota(jnp.int32, (GATE, GATE), 1)).astype(bf16)


def turned(left, right):
    return lax.dot_general(left, right, (((1,), (1,)), ((), ())), preferred_element_type=f32)


def chosen(one_hot, gate):
    return [turned(turned(one_hot, part).astype(bf16), one_hot).astype(bf16) for part in halves(gate)]


def unit_turn(quarters):
    whole = jnp.floor(quarters + 0.5)
    r = (quarters - whole) * 1.5707963267948966
    s = r * r
    sine = r + r * s * (-1.6666654611e-1 + s * (8.3321608736e-3 - s * 1.9515295891e-4))
    cosine = 1.0 - 0.5 * s + s * s * (
        4.166664568298827e-2 + s * (-1.388731625493765e-3 + s * 2.443315711809948e-5)
    )
    quarter = whole.astype(jnp.int32)
    swap = (quarter & 1) == 1
    base_sin = jnp.where(swap, cosine, sine)
    base_cos = jnp.where(swap, sine, cosine)
    sine = jnp.where((quarter & 2) == 2, -base_sin, base_sin)
    cosine = jnp.where(((quarter + 1) & 2) == 2, -base_cos, base_cos)
    return cosine, sine


def moves(pairs, sems):
    return [pltpu.make_async_copy(a, b, sems.at[i]) for i, (a, b) in enumerate(pairs)]


def front_kernel(base_ref, orders_ref, masks_ref, angles_ref, real_ref, imag_ref, gates_ref,
                 send_ref, gate_ref, need_ref, weight_ref, table_ref, place_ref,
                 in_ref, out_ref, in_sems, out_sems):
    top, total = real_ref.shape[:2]
    count = FRONT_ROWS
    chunks = total // count
    pairs = masks_ref.shape[1]
    patterns = 2**pairs
    rows = top * count
    order = range(top)
    spans = [pl.ds(chunk * count, count) for chunk in range(chunks)]
    arrive = moves(
        [
            (ref.at[:, span], in_ref.at[part, :, span])
            for span in spans
            for part, ref in enumerate((real_ref, imag_ref))
        ],
        in_sems,
    )
    leave = moves([(out_ref.at[span], send_ref.at[span]) for span in spans], out_sems)
    for copy in arrive:
        copy.start()

    states = lax.broadcasted_iota(jnp.int32, (GATE, GATE), 0)
    one_hot = pick(states, orders_ref, 0)
    real_high, real_low = chosen(one_hot, gates_ref[0, 0])
    imag_high, imag_low = chosen(one_hot, gates_ref[0, 1])
    for spot, real, imag in (
        (0, real_high, imag_high),
        (2, real_low, imag_low),
        (4, real_high, imag_high),
    ):
        upper = slice(spot * GATE, (spot + 1) * GATE)
        lower = slice((spot + 1) * GATE, (spot + 2) * GATE)
        gate_ref[upper, :GATE] = real
        gate_ref[lower, :GATE] = -imag
        gate_ref[upper, GATE:] = imag
        gate_ref[lower, GATE:] = real
    lane = lax.broadcasted_iota(jnp.int32, (8, GATE), 1)
    spot = lax.broadcasted_iota(jnp.int32, (GATE, GATE), 0)
    column = lax.broadcasted_iota(jnp.int32, (patterns, GATE), 1)
    pattern = lax.broadcasted_iota(jnp.int32, (patterns, GATE), 0)
    need = jnp.zeros((8, GATE), jnp.int32) - 1
    weight = jnp.zeros((GATE, GATE), f32)
    quarters = jnp.zeros((patterns, GATE), f32)
    for pair in range(pairs):
        mask = masks_ref[0, pair] | masks_ref[1, pair]
        inside = mask & (GATE - 1)
        need = jnp.where(lane == pair, mask & ~(GATE - 1), need)
        weight = jnp.where(spot == pair, float(2**pair), weight)
        met = ((column & inside) == inside) & (((pattern >> pair) & 1) == 1)
        quarters = quarters + jnp.where(met, angles_ref[pair] * 0.6366197723675814, 0.0)
    need_ref[...] = need
    weight_ref[...] = weight.astype(bf16)
    for half, value in enumerate(unit_turn(quarters)):
        lanes = slice(half * GATE, (half + 1) * GATE)
        table_ref[:patterns, lanes], table_ref[patterns:, lanes] = halves(value)
    within = lax.broadcasted_iota(jnp.int32, (count, GATE), 0) * GATE
    for spot, high in enumerate(order):
        place_ref[spot] = within + (base_ref[0] + high * (256 * GATE))

    need = need_ref[0:1, :]
    lane = lax.broadcasted_iota(jnp.int32, (rows, GATE), 1).astype(f32)
    for chunk in range(chunks):
        span = slice(chunk * count, (chunk + 1) * count)
        arrive[2 * chunk].wait()
        arrive[2 * chunk + 1].wait()
        both = jnp.concatenate(
            [in_ref[part, :, span].reshape(rows, GATE) for part in range(2)], axis=1
        )
        x_high, x_low = halves(both)
        new = mul(jnp.concatenate([x_high, x_high, x_low], axis=1), gate_ref[...])
        flat = place_ref[...].reshape(rows, GATE) + chunk * (count * GATE)
        conditions = jnp.where((flat & need) == need, 1.0, 0.0).astype(bf16)
        found = mul(conditions, weight_ref[...])
        chosen_rows = [
            jnp.where(found == lane + float(first), 1.0, 0.0).astype(bf16)
            for first in range(0, patterns, GATE)
        ]
        turn = mul(jnp.concatenate(chosen_rows * 2, axis=1), table_ref[...])
        cosine, sine = turn[:, :GATE], turn[:, GATE:]
        real = new[:, :GATE]
        imag = new[:, GATE:]
        for part, value in enumerate((real * cosine - imag * sine, real * sine + imag * cosine)):
            out_ref[span, part] = jnp.transpose(value.reshape(top, count, GATE), (1, 0, 2))
        leave[chunk].start()
    for copy in leave:
        copy.wait()


def middle_kernel(second_ref, third_ref, got_ref, back_ref, gates_ref, mid_ref,
                  in_ref, out_ref, in_sems, out_sems):
    inputs, outputs = got_ref.shape[:2]
    apart = outputs // GATE_STEPS
    wide_apart = inputs // BACK_STEPS
    spans = [pl.ds(chunk * apart, apart) for chunk in range(GATE_STEPS)]
    arrive = moves([(got_ref.at[:, span], in_ref.at[:, span]) for span in spans], in_sems)
    spans = [pl.ds(chunk * wide_apart, wide_apart) for chunk in range(BACK_STEPS)]
    leave = moves([(out_ref.at[span], back_ref.at[span]) for span in spans], out_sems)
    for copy in arrive:
        copy.start()
    for which, ref in enumerate((second_ref, third_ref)):
        high, low = halves(ref[...])
        gates_ref[which] = jnp.concatenate([high, low], axis=0)

    def apply(which, x):
        x_high, x_low = halves(x)
        first = mul(gates_ref[which], x_high)
        return first[:256] + first[256:] + mul(gates_ref[which, :256], x_low)

    for narrow in range(outputs):
        if narrow % apart == 0:
            arrive[narrow // apart].wait()
        parts = [jnp.transpose(in_ref[:, narrow, part], (1, 0, 2)) for part in range(2)]
        columns = [
            jnp.concatenate([part[inner * 4 + rest] for part in parts for inner in range(4)], axis=0)
            for rest in range(4)
        ]
        out = apply(0, jnp.concatenate(columns, axis=1))
        for part in range(2):
            stack = jnp.stack(
                [
                    out[
                        part * GATE + inner * inputs : part * GATE + (inner + 1) * inputs,
                        rest * GATE : (rest + 1) * GATE,
                    ]
                    for rest in range(4)
                    for inner in range(4)
                ],
                axis=0,
            )
            mid_ref[part, :, narrow] = jnp.transpose(stack, (1, 0, 2))
    for group in range(inputs // 4):
        first = group * 4
        columns = [
            jnp.concatenate(
                [mid_ref[part, first + wide].reshape(GATE, GATE) for part in range(2)], axis=0
            )
            for wide in range(4)
        ]
        out = apply(1, jnp.concatenate(columns, axis=1))
        for wide in range(4):
            out_ref[first + wide] = out[:, wide * GATE : (wide + 1) * GATE].reshape(
                outputs, 2, 16, GATE
            )
        if (first + 4) % wide_apart == 0:
            leave[first // wide_apart].start()
    for copy in leave:
        copy.wait()


def last_kernel(got_ref, real_ref, imag_ref, in_ref, out_ref, in_sems, out_sems):
    chunks = got_ref.shape[0] // LAST_ROWS
    spans = [pl.ds(chunk * LAST_ROWS, LAST_ROWS) for chunk in range(chunks)]
    arrive = moves([(got_ref.at[span], in_ref.at[span]) for span in spans], in_sems)
    leave = moves(
        [
            (out_ref.at[part, :, span], ref.at[:, span])
            for span in spans
            for part, ref in enumerate((real_ref, imag_ref))
        ],
        out_sems,
    )
    for copy in arrive:
        copy.start()
    for chunk in range(chunks):
        span = slice(chunk * LAST_ROWS, (chunk + 1) * LAST_ROWS)
        arrive[chunk].wait()
        for part in range(2):
            out_ref[part, :, span] = jnp.transpose(in_ref[span, part], (1, 0, 2))
            leave[2 * chunk + part].start()
    for copy in leave:
        copy.wait()


def ordered(gate_pair, order_row, row_states, column_states):
    def one_hot(states):
        places = jnp.arange(QUBITS, dtype=jnp.int32)
        digits = states[:, None] >> places[None, :] & 1
        mapped = jnp.sum(digits << order_row[None, :], axis=1)
        return (mapped[:, None] == jnp.arange(GATE, dtype=jnp.int32)[None, :]).astype(f32)

    precise = lax.Precision.HIGHEST
    left, right = one_hot(row_states), one_hot(column_states)
    return [
        jnp.dot(jnp.dot(left, part, precision=precise), right.T, precision=precise)
        for part in (gate_pair[0], gate_pair[1])
    ]


def body(state_real, state_imag, gates, gate_orders, phase_masks, phase_angles):
    real_part = state_real[0, 0]
    imag_part = state_imag[0, 0]
    rows, columns = real_part.shape
    wide_count = lax.axis_size("wide")
    narrow_count = lax.axis_size("narrow")
    devices = wide_count * narrow_count
    base = (lax.axis_index("narrow") * wide_count + lax.axis_index("wide")) * (rows * columns)
    packed = jax.ShapeDtypeStruct((devices, 2, 16, columns), f32)
    tall = jax.ShapeDtypeStruct((16, devices, columns), f32)
    count = FRONT_ROWS
    send = pl.pallas_call(
        front_kernel,
        out_shape=packed,
        in_specs=[SMEM] * 4 + [ANY, ANY, VMEM],
        out_specs=ANY,
        scratch_shapes=[
            pltpu.VMEM((768, 256), bf16),
            pltpu.VMEM((8, GATE), jnp.int32),
            pltpu.VMEM((GATE, GATE), bf16),
            pltpu.VMEM((2 * 2 ** phase_masks.shape[0], 256), bf16),
            pltpu.VMEM((16, count, GATE), jnp.int32),
            pltpu.VMEM((2, 16, devices, columns), f32),
            pltpu.VMEM((devices, 2, 16, columns), f32),
            DMA((2 * devices // count,)),
            DMA((devices // count,)),
        ],
        name="front",
    )(
        base[None],
        gate_orders,
        phase_masks.T,
        phase_angles,
        real_part.reshape(16, devices, columns),
        imag_part.reshape(16, devices, columns),
        gates,
    )

    def exchange(block):
        return lax.all_to_all(block, AXES, split_axis=0, concat_axis=0, tiled=True)

    got = exchange(send)
    states = jnp.arange(GATE, dtype=jnp.int32)
    by_inner = states % 32 * 4 + states // 32
    second = ordered(gates[1], gate_orders[1], by_inner, by_inner)
    swapped = states // 16 * 16 + states % 4 * 4 + states // 4 % 4
    third = ordered(gates[2], gate_orders[2], states, swapped)
    second = jnp.concatenate(
        [
            jnp.concatenate([second[0], -second[1]], axis=1),
            jnp.concatenate([second[1], second[0]], axis=1),
        ],
        axis=0,
    )
    third = jnp.stack(
        [
            jnp.concatenate([third[0], -third[1]], axis=1).reshape(8, 16, 256),
            jnp.concatenate([third[1], third[0]], axis=1).reshape(8, 16, 256),
        ],
        axis=1,
    ).reshape(256, 256)
    back = pl.pallas_call(
        middle_kernel,
        out_shape=jax.ShapeDtypeStruct((wide_count, narrow_count, 2, 16, columns), f32),
        in_specs=[VMEM, VMEM, ANY],
        out_specs=ANY,
        scratch_shapes=[
            pltpu.VMEM((2, 512, 256), bf16),
            pltpu.VMEM((2, wide_count, narrow_count, 16, columns), f32),
            pltpu.VMEM((wide_count, narrow_count, 2, 16, columns), f32),
            pltpu.VMEM((wide_count, narrow_count, 2, 16, columns), f32),
            DMA((GATE_STEPS,)),
            DMA((BACK_STEPS,)),
        ],
        name="middle",
    )(second, third, got.reshape(wide_count, narrow_count, 2, 16, columns))
    final = exchange(back.reshape(devices, 2, 16, columns))
    out_real, out_imag = pl.pallas_call(
        last_kernel,
        out_shape=(tall, tall),
        in_specs=[ANY],
        out_specs=(ANY, ANY),
        scratch_shapes=[
            pltpu.VMEM((devices, 2, 16, columns), f32),
            pltpu.VMEM((2, 16, devices, columns), f32),
            DMA((devices // LAST_ROWS,)),
            DMA((2 * devices // LAST_ROWS,)),
        ],
        name="last",
    )(final)
    out_real, out_imag = out_real.reshape(rows, columns), out_imag.reshape(rows, columns)
    return (out_real[None, None], out_imag[None, None])


def solution(mesh):
    placed = (P("narrow", "wide", None, None), P("narrow", "wide", None, None), P(), P(), P(), P())
    return jax.shard_map(
        body,
        mesh=mesh,
        in_specs=placed,
        out_specs=(P("narrow", "wide", None, None), P("narrow", "wide", None, None)),
        check_vma=False,
    )
```

```python
import functools

import jax
import jax.numpy as jnp
from jax import lax
from jax.experimental import pallas as pl
from jax.experimental.pallas import tpu as pltpu
from jax.sharding import PartitionSpec as P

AXES = ("wide", "narrow")
QUBITS = 7
FRONT_ROWS = 64
LAST_ROWS = 64
GATE_STEPS = 2
GATE = 128
f32 = jnp.float32
bf16 = jnp.bfloat16
VMEM = pl.BlockSpec(memory_space=pltpu.VMEM)
SMEM = pl.BlockSpec(memory_space=pltpu.SMEM)
ANY = pl.BlockSpec(memory_space=pl.ANY)
DMA = pltpu.SemaphoreType.DMA


def halves(value):
    high = value.astype(bf16)
    return high, (value - high.astype(f32)).astype(bf16)


def mul(left, right):
    return jnp.dot(left, right, preferred_element_type=f32)


def pick(states, orders_ref, row):
    mapped = jnp.zeros_like(states)
    for place in range(QUBITS):
        mapped = mapped + (((states >> place) & 1) << orders_ref[row, place])
    return (mapped == lax.broadcasted_iota(jnp.int32, (GATE, GATE), 1)).astype(bf16)


def turned(left, right):
    return lax.dot_general(left, right, (((1,), (1,)), ((), ())), preferred_element_type=f32)


def chosen(one_hot, gate):
    return [turned(turned(one_hot, part).astype(bf16), one_hot).astype(bf16) for part in halves(gate)]


def unit_turn(quarters):
    whole = jnp.floor(quarters + 0.5)
    r = (quarters - whole) * 1.5707963267948966
    s = r * r
    sine = r + r * s * (-1.6666654611e-1 + s * (8.3321608736e-3 - s * 1.9515295891e-4))
    cosine = 1.0 - 0.5 * s + s * s * (
        4.166664568298827e-2 + s * (-1.388731625493765e-3 + s * 2.443315711809948e-5)
    )
    quarter = whole.astype(jnp.int32)
    swap = (quarter & 1) == 1
    base_sin = jnp.where(swap, cosine, sine)
    base_cos = jnp.where(swap, sine, cosine)
    sine = jnp.where((quarter & 2) == 2, -base_sin, base_sin)
    cosine = jnp.where(((quarter + 1) & 2) == 2, -base_cos, base_cos)
    return cosine, sine


def moves(pairs, sems):
    return [pltpu.make_async_copy(a, b, sems.at[i]) for i, (a, b) in enumerate(pairs)]


def front_kernel(base_ref, orders_ref, masks_ref, angles_ref, real_ref, imag_ref, gates_ref,
                 send_ref, gate_ref, need_ref, weight_ref, table_ref, place_ref,
                 in_ref, out_ref, in_sems, out_sems):
    top, total = real_ref.shape[:2]
    count = FRONT_ROWS
    chunks = total // count
    pairs = masks_ref.shape[1]
    patterns = 2**pairs
    rows = top * count
    order = range(top)
    spans = [pl.ds(chunk * count, count) for chunk in range(chunks)]
    arrive = moves(
        [
            (ref.at[:, span], in_ref.at[part, :, span])
            for span in spans
            for part, ref in enumerate((real_ref, imag_ref))
        ],
        in_sems,
    )
    leave = moves([(out_ref.at[span], send_ref.at[span]) for span in spans], out_sems)
    for copy in arrive:
        copy.start()

    states = lax.broadcasted_iota(jnp.int32, (GATE, GATE), 0)
    one_hot = pick(states, orders_ref, 0)
    real_high, real_low = chosen(one_hot, gates_ref[0, 0])
    imag_high, imag_low = chosen(one_hot, gates_ref[0, 1])
    for spot, real, imag in (
        (0, real_high, imag_high),
        (2, real_low, imag_low),
        (4, real_high, imag_high),
    ):
        upper = slice(spot * GATE, (spot + 1) * GATE)
        lower = slice((spot + 1) * GATE, (spot + 2) * GATE)
        gate_ref[upper, :GATE] = real
        gate_ref[lower, :GATE] = -imag
        gate_ref[upper, GATE:] = imag
        gate_ref[lower, GATE:] = real
    lane = lax.broadcasted_iota(jnp.int32, (8, GATE), 1)
    spot = lax.broadcasted_iota(jnp.int32, (GATE, GATE), 0)
    column = lax.broadcasted_iota(jnp.int32, (patterns, GATE), 1)
    pattern = lax.broadcasted_iota(jnp.int32, (patterns, GATE), 0)
    need = jnp.zeros((8, GATE), jnp.int32) - 1
    weight = jnp.zeros((GATE, GATE), f32)
    quarters = jnp.zeros((patterns, GATE), f32)
    for pair in range(pairs):
        mask = masks_ref[0, pair] | masks_ref[1, pair]
        inside = mask & (GATE - 1)
        need = jnp.where(lane == pair, mask & ~(GATE - 1), need)
        weight = jnp.where(spot == pair, float(2**pair), weight)
        met = ((column & inside) == inside) & (((pattern >> pair) & 1) == 1)
        quarters = quarters + jnp.where(met, angles_ref[pair] * 0.6366197723675814, 0.0)
    need_ref[...] = need
    weight_ref[...] = weight.astype(bf16)
    for half, value in enumerate(unit_turn(quarters)):
        lanes = slice(half * GATE, (half + 1) * GATE)
        table_ref[:patterns, lanes], table_ref[patterns:, lanes] = halves(value)
    within = lax.broadcasted_iota(jnp.int32, (count, GATE), 0) * GATE
    for spot, high in enumerate(order):
        place_ref[spot] = within + (base_ref[0] + high * (256 * GATE))

    need = need_ref[0:1, :]
    lane = lax.broadcasted_iota(jnp.int32, (rows, GATE), 1).astype(f32)
    for chunk in range(chunks):
        span = slice(chunk * count, (chunk + 1) * count)
        arrive[2 * chunk].wait()
        arrive[2 * chunk + 1].wait()
        both = jnp.concatenate(
            [in_ref[part, :, span].reshape(rows, GATE) for part in range(2)], axis=1
        )
        x_high, x_low = halves(both)
        new = mul(jnp.concatenate([x_high, x_high, x_low], axis=1), gate_ref[...])
        flat = place_ref[...].reshape(rows, GATE) + chunk * (count * GATE)
        conditions = jnp.where((flat & need) == need, 1.0, 0.0).astype(bf16)
        found = mul(conditions, weight_ref[...])
        chosen_rows = [
            jnp.where(found == lane + float(first), 1.0, 0.0).astype(bf16)
            for first in range(0, patterns, GATE)
        ]
        turn = mul(jnp.concatenate(chosen_rows * 2, axis=1), table_ref[...])
        cosine, sine = turn[:, :GATE], turn[:, GATE:]
        real = new[:, :GATE]
        imag = new[:, GATE:]
        for part, value in enumerate((real * cosine - imag * sine, real * sine + imag * cosine)):
            out_ref[span, part] = jnp.transpose(value.reshape(top, count, GATE), (1, 0, 2))
        leave[chunk].start()
    for copy in leave:
        copy.wait()


def middle_kernel(second_ref, third_ref, got_ref, back_ref, mid_ref, gates_ref):
    step = pl.program_id(0)
    inputs, together = got_ref.shape[:2]
    steps = 8 // together

    @pl.when(step == 0)
    def _():
        for which, ref in enumerate((second_ref, third_ref)):
            high, low = halves(ref[...])
            gates_ref[which] = jnp.concatenate([high, low, high], axis=1)

    def apply(which, x):
        x_high, x_low = halves(x)
        return mul(gates_ref[which], jnp.concatenate([x_high, x_high, x_low], axis=0))

    @pl.when(step < steps)
    def _():
        for narrow in range(together):
            parts = [jnp.transpose(got_ref[:, narrow, part], (1, 0, 2)) for part in range(2)]
            columns = [
                jnp.concatenate(
                    [part[inner * 4 + rest] for part in parts for inner in range(4)], axis=0
                )
                for rest in range(4)
            ]
            out = apply(0, jnp.concatenate(columns, axis=1))
            for part in range(2):
                stack = jnp.stack(
                    [
                        out[
                            part * GATE + inner * inputs : part * GATE + (inner + 1) * inputs,
                            rest * GATE : (rest + 1) * GATE,
                        ]
                        for rest in range(4)
                        for inner in range(4)
                    ],
                    axis=0,
                )
                mid_ref[part, :, step * together + narrow] = jnp.transpose(stack, (1, 0, 2))

    @pl.when(step >= steps)
    def _():
        count = back_ref.shape[0]

        for group in range(count // 4):
            first = (step - steps) * count + group * 4
            columns = [
                jnp.concatenate(
                    [mid_ref[part, first + wide].reshape(GATE, GATE) for part in range(2)], axis=0
                )
                for wide in range(4)
            ]
            out = apply(1, jnp.concatenate(columns, axis=1))
            for wide in range(4):
                back_ref[group * 4 + wide] = out[:, wide * GATE : (wide + 1) * GATE].reshape(
                    8, 2, 16, GATE
                )


def last_kernel(got_ref, real_ref, imag_ref, in_ref, out_ref, in_sems, out_sems):
    chunks = got_ref.shape[0] // LAST_ROWS
    spans = [pl.ds(chunk * LAST_ROWS, LAST_ROWS) for chunk in range(chunks)]
    arrive = moves([(got_ref.at[span], in_ref.at[span]) for span in spans], in_sems)
    leave = moves(
        [
            (out_ref.at[part, :, span], ref.at[:, span])
            for span in spans
            for part, ref in enumerate((real_ref, imag_ref))
        ],
        out_sems,
    )
    for copy in arrive:
        copy.start()
    for chunk in range(chunks):
        span = slice(chunk * LAST_ROWS, (chunk + 1) * LAST_ROWS)
        arrive[chunk].wait()
        for part in range(2):
            out_ref[part, :, span] = jnp.transpose(in_ref[span, part], (1, 0, 2))
            leave[2 * chunk + part].start()
    for copy in leave:
        copy.wait()


def ordered(gate_pair, order_row, row_states, column_states):
    def one_hot(states):
        places = jnp.arange(QUBITS, dtype=jnp.int32)
        digits = states[:, None] >> places[None, :] & 1
        mapped = jnp.sum(digits << order_row[None, :], axis=1)
        return (mapped[:, None] == jnp.arange(GATE, dtype=jnp.int32)[None, :]).astype(f32)

    precise = lax.Precision.HIGHEST
    left, right = one_hot(row_states), one_hot(column_states)
    return [
        jnp.dot(jnp.dot(left, part, precision=precise), right.T, precision=precise)
        for part in (gate_pair[0], gate_pair[1])
    ]


def body(state_real, state_imag, gates, gate_orders, phase_masks, phase_angles):
    real_part = state_real[0, 0]
    imag_part = state_imag[0, 0]
    rows, columns = real_part.shape
    wide_count = lax.axis_size("wide")
    narrow_count = lax.axis_size("narrow")
    devices = wide_count * narrow_count
    base = (lax.axis_index("narrow") * wide_count + lax.axis_index("wide")) * (rows * columns)
    packed = jax.ShapeDtypeStruct((devices, 2, 16, columns), f32)
    tall = jax.ShapeDtypeStruct((16, devices, columns), f32)
    count = FRONT_ROWS
    send = pl.pallas_call(
        front_kernel,
        out_shape=packed,
        in_specs=[SMEM] * 4 + [ANY, ANY, VMEM],
        out_specs=ANY,
        scratch_shapes=[
            pltpu.VMEM((768, 256), bf16),
            pltpu.VMEM((8, GATE), jnp.int32),
            pltpu.VMEM((GATE, GATE), bf16),
            pltpu.VMEM((2 * 2 ** phase_masks.shape[0], 256), bf16),
            pltpu.VMEM((16, count, GATE), jnp.int32),
            pltpu.VMEM((2, 16, devices, columns), f32),
            pltpu.VMEM((devices, 2, 16, columns), f32),
            DMA((2 * devices // count,)),
            DMA((devices // count,)),
        ],
        name="front",
    )(
        base[None],
        gate_orders,
        phase_masks.T,
        phase_angles,
        real_part.reshape(16, devices, columns),
        imag_part.reshape(16, devices, columns),
        gates,
    )

    def exchange(block):
        return lax.all_to_all(block, AXES, split_axis=0, concat_axis=0, tiled=True)

    got = exchange(send)
    states = jnp.arange(GATE, dtype=jnp.int32)
    by_inner = states % 32 * 4 + states // 32
    second = ordered(gates[1], gate_orders[1], by_inner, by_inner)
    swapped = states // 16 * 16 + states % 4 * 4 + states // 4 % 4
    third = ordered(gates[2], gate_orders[2], states, swapped)
    second = jnp.concatenate(
        [
            jnp.concatenate([second[0], -second[1]], axis=1),
            jnp.concatenate([second[1], second[0]], axis=1),
        ],
        axis=0,
    )
    third = jnp.stack(
        [
            jnp.concatenate([third[0], -third[1]], axis=1).reshape(8, 16, 256),
            jnp.concatenate([third[1], third[0]], axis=1).reshape(8, 16, 256),
        ],
        axis=1,
    ).reshape(256, 256)
    back = pl.pallas_call(
        middle_kernel,
        out_shape=jax.ShapeDtypeStruct((wide_count, narrow_count, 2, 16, columns), f32),
        grid=(GATE_STEPS * 2,),
        in_specs=[
            VMEM,
            VMEM,
            pl.BlockSpec(
                (wide_count, narrow_count // GATE_STEPS, 2, 16, columns),
                lambda i: (0, jnp.minimum(i, GATE_STEPS - 1), 0, 0, 0),
            ),
        ],
        out_specs=pl.BlockSpec(
            (wide_count // GATE_STEPS, narrow_count, 2, 16, columns),
            lambda i: (jnp.maximum(i - GATE_STEPS, 0), 0, 0, 0, 0),
        ),
        scratch_shapes=[
            pltpu.VMEM((2, wide_count, narrow_count, 16, columns), f32),
            pltpu.VMEM((2, 256, 768), bf16),
        ],
        name="middle",
    )(second, third, got.reshape(wide_count, narrow_count, 2, 16, columns))
    final = exchange(back.reshape(devices, 2, 16, columns))
    out_real, out_imag = pl.pallas_call(
        last_kernel,
        out_shape=(tall, tall),
        in_specs=[ANY],
        out_specs=(ANY, ANY),
        scratch_shapes=[
            pltpu.VMEM((devices, 2, 16, columns), f32),
            pltpu.VMEM((2, 16, devices, columns), f32),
            DMA((devices // LAST_ROWS,)),
            DMA((2 * devices // LAST_ROWS,)),
        ],
        name="last",
    )(final)
    out_real, out_imag = out_real.reshape(rows, columns), out_imag.reshape(rows, columns)
    return (out_real[None, None], out_imag[None, None])


def solution(mesh):
    placed = (P("narrow", "wide", None, None), P("narrow", "wide", None, None), P(), P(), P(), P())
    return jax.shard_map(
        body,
        mesh=mesh,
        in_specs=placed,
        out_specs=(P("narrow", "wide", None, None), P("narrow", "wide", None, None)),
        check_vma=False,
    )
```
